32 devices in a mesh: site: 4 (over z), bond: 8 (over y, x, core).
Axes of the slice: x: 2, y: 2, z: 4, core: 2. Of those that a mesh axis runs over, the one named last changes fastest.
Arguments:
- site_tensor: float32 [4, 4, 3072, 3072], P('site', None, 'bond'), may hold values from -0.15625 to 0.15625
- panels: float32 [4, 3072, 128], P('site', 'bond'), may hold values from -6 to 6
- fresh: float32 [1, 3072, 128], P(None, 'bond'), may hold values from -6 to 6
- outcomes: int32 [4, 2, 128], P('site'), may hold values from 0 to 3, as said below
Outputs:
- carried: float32 [4, 2, 3072, 128], P('site', None, 'bond')
The draws below stay inside these ranges and needn't reach their ends.
Inputs may be any that keep to these rules, and one draw needn't show every extreme that they name: `outcomes`: at each site and tick, every outcome is taken by at most 48 samples, and some outcome by exactly 48.
All inputs are finite; a program needn't handle non-finite values.
Results may differ from the reference program's by a relative error of at most 0.0001.
Values sent between devices are 32-bit elements; how exact they have to be, the bound alone decides.
A program may use at most 64 MiB of HBM per device.

```python
import jax
import jax.numpy as jnp
from jax import lax

CHI = 3072
OUTCOMES = 4
SAMPLES = 128
TICKS = 2
SITES = 4


def draw_outcomes(key, part):
    site_keys = jax.random.split(jax.random.fold_in(key, 7), SITES * TICKS)

    def draw_single(one_key):
        key_first, key_second, key_order, key_shuffle = jax.random.split(one_key, 4)
        most_count = SAMPLES * 3 // 8
        remaining = SAMPLES - most_count
        count_first = jax.random.randint(key_first, (), 0, most_count + 1)
        lower_bound = jnp.maximum(0, remaining - count_first - most_count)
        upper_bound = jnp.minimum(most_count, remaining - count_first)
        count_second = jax.random.randint(key_second, (), lower_bound, upper_bound + 1)
        count_third = remaining - count_first - count_second
        counts_all = jnp.stack([jnp.int32(most_count), count_first.astype(jnp.int32), count_second.astype(jnp.int32), count_third.astype(jnp.int32)])
        outcome_order = jax.random.permutation(key_order, 4).astype(jnp.int32)
        boundaries = jnp.cumsum(counts_all)
        position = jnp.arange(SAMPLES, dtype=jnp.int32)
        bucket_slot = jnp.sum((position[:, None] >= boundaries[None, :]).astype(jnp.int32), axis=1)
        labelled = outcome_order[bucket_slot]
        return jax.random.permutation(key_shuffle, labelled).astype(jnp.int32)
    return jax.vmap(draw_single)(site_keys).reshape(SITES, TICKS, SAMPLES)


def strengthened(drawn, key, source, target, shards_of, factor):
    def block_of(axis_at):
        return (jnp.arange(drawn.shape[axis_at]) // (drawn.shape[axis_at] // shards_of)).reshape((-1,) + (1,) * (drawn.ndim - 1 - axis_at))

    near = jax.random.permutation(key, shards_of)[block_of(target)]
    far = (block_of(target) + shards_of // 2) % shards_of
    return jnp.where((block_of(source) == near) | (block_of(source) == far), factor * drawn, drawn)


def shard_levels(own_key, dims, pieces, low, high):
    gain = 1.0
    for axis_at, parts in pieces:
        draws = jax.random.uniform(jax.random.fold_in(jax.random.fold_in(own_key, 6), axis_at), (parts,), jnp.float32, low / len(pieces), high / len(pieces))
        gain = gain * jnp.repeat(jnp.exp(draws), dims[axis_at] // parts).reshape((-1,) + (1,) * (len(dims) - 1 - axis_at))
    return gain


def scatter_about(stream_key, extent, scale, reach, shards=(), kind=jnp.bfloat16):
    entries = scale * jax.random.normal(stream_key, extent, jnp.float32)
    if shards:
        entries = entries * shard_levels(stream_key, extent, shards, -0.22, 0.18)
    return jnp.clip(entries, -reach, reach).astype(kind)


def noise_with(own_key, dims, width, limit, cuts, heavy, kind=jnp.bfloat16):
    array = width * jax.random.normal(own_key, dims, jnp.float32)
    if cuts:
        array = array * shard_levels(own_key, dims, cuts, -0.22, 0.18)
    return jnp.clip(strengthened(array, jax.random.fold_in(own_key, 3), *heavy), -limit, limit).astype(kind)


def setup_inputs(seed: int = 0) -> dict:
    splits = jax.random.split(jax.random.key(seed), 5)
    return {
        "site_tensor": noise_with(splits[0], (SITES, OUTCOMES, CHI, CHI), CHI ** -0.5, 0.15625, ((0, 4), (2, 8)), (2, 3, 8, 2.0), jnp.float32),
        "panels": scatter_about(splits[1], (SITES, CHI, SAMPLES), 1.0, 6.0, ((0, 4), (1, 8)), jnp.float32),
        "fresh": scatter_about(splits[2], (TICKS - 1, CHI, SAMPLES), 1.0, 6.0, ((1, 8),), jnp.float32),
        "outcomes": draw_outcomes(jax.random.fold_in(splits[4], 71), 0),
    }


def advance(tensor, vectors, selected):
    accumulated = jnp.zeros((tensor.shape[2], vectors.shape[1]), jnp.float32)
    for outcome_index in range(tensor.shape[0]):
        column_mask = (selected == outcome_index).astype(jnp.float32)
        masked = vectors * column_mask[None, :]
        accumulated = accumulated + jnp.dot(tensor[outcome_index].T, masked, precision=lax.Precision.HIGHEST, preferred_element_type=jnp.float32)
    return accumulated


def reference(site_tensor, panels, fresh, outcomes):
    current = panels
    results = []
    for tick_index in range(TICKS):
        produced = []
        for site_index in range(SITES):
            produced.append(advance(site_tensor[site_index], current[site_index], outcomes[site_index, tick_index]))
        stacked = jnp.stack(produced, 0)
        results.append(stacked)
        if tick_index + 1 < TICKS:
            current = jnp.concatenate([fresh[tick_index][None], stacked[:-1]], 0)
    return jnp.stack(results, 1)
```

```python
import functools
import math

import jax
import jax.numpy as jnp
from jax import lax
from jax.experimental import pallas as pl
from jax.experimental.pallas import tpu as pltpu
from jax.sharding import PartitionSpec as P

TILE = 256


def flipped(index, mask):
    result = index
    bit = 0
    while (1 << bit) <= mask:
        if mask >> bit & 1:
            result = result + (1 - 2 * ((index // (1 << bit)) % 2)) * (1 << bit)
        bit += 1
    return result


def kernel(
    plan,
    tensor_ref,
    panel_ref,
    fresh_ref,
    outcome_ref,
    out_ref,
    raw,
    high,
    low,
    stacked,
    left,
    part,
    core_in,
    stage_in,
    hop_in,
    load_sem,
    core_send,
    core_recv,
    stage_send,
    stage_recv,
    hop_send,
    hop_recv,
):
    sites, bond, ticks, count, rows, samples, chunk, width = plan
    bits = bond.bit_length() - 1
    uppers = 1 << (bits - 1)
    per_block = width // chunk
    blocks = bond // per_block
    tiles = width // TILE
    half = chunk // 2
    orders = (tuple(range(1, bits)), tuple(reversed(range(1, bits))))

    me = lax.axis_index("bond")
    site = lax.axis_index("site")

    def at(bond_mask):
        return {"bond": flipped(me, bond_mask)}

    def load(step, tile):
        block = flipped(me // per_block, blocks - 1 - step)
        column = pl.multiple_of(block * width + tile * TILE, TILE)
        return pltpu.make_async_copy(
            tensor_ref.at[0, :, :, pl.ds(column, TILE)],
            raw.at[step * tiles + tile],
            load_sem.at[step * tiles + tile],
        )

    for step in range(blocks):
        for tile in range(tiles):
            load(step, tile).start()

    barrier = pltpu.get_barrier_semaphore()
    for bit in range(bits):
        pl.semaphore_signal(
            barrier, inc=1, device_id=at(1 << bit), device_id_type=pl.DeviceIdType.MESH
        )

    @pl.when(site > 0)
    def _():
        pl.semaphore_signal(
            barrier, inc=1, device_id={"site": site - 1}, device_id_type=pl.DeviceIdType.MESH
        )

    @pl.when(site < sites - 1)
    def _():
        pl.semaphore_signal(
            barrier, inc=1, device_id={"site": site + 1}, device_id_type=pl.DeviceIdType.MESH
        )

    def prepare(vectors, tick):
        chosen = outcome_ref[0, pl.ds(tick, 1), :]
        for outcome in range(count):
            stacked[pl.ds(outcome * rows, rows), :] = jnp.where(chosen == outcome, vectors, 0.0)
        turned = stacked[...].T
        upper = turned.astype(jnp.bfloat16)
        left[pl.ds(0, samples), :] = upper
        left[pl.ds(samples, samples), :] = (turned - upper.astype(jnp.float32)).astype(jnp.bfloat16)

    def compute(tick, step):
        def one(tile):
            index = step * tiles + tile
            if tick == 0:
                load(step, tile).wait()
                for outcome in range(count):
                    values = raw[index, outcome]
                    upper = values.astype(jnp.bfloat16)
                    high[index, pl.ds(outcome * rows, rows), :] = upper
                    low[index, pl.ds(outcome * rows, rows), :] = (
                        values - upper.astype(jnp.float32)
                    ).astype(jnp.bfloat16)
            both = jnp.dot(left[...], high[index], preferred_element_type=jnp.float32)
            rest = jnp.dot(
                left[pl.ds(0, samples), :], low[index], preferred_element_type=jnp.float32
            )
            total = both[:samples] + (both[samples:] + rest)
            part[tick, step, pl.ds(pl.multiple_of(tile * TILE, TILE), TILE), :] = total.T

        if plan_unroll:
            for tile in range(tiles):
                one(tile)
        else:
            lax.fori_loop(0, tiles, lambda tile, _: (one(tile), 0)[1], 0)

    plan_unroll = True

    def place(rel):
        step = blocks - 1 - rel // per_block
        offset = flipped(me % per_block, rel % per_block) * chunk
        return step, offset

    def rows_of(tick, rel, start, size):
        step, offset = place(rel)
        return part.at[tick, step, pl.ds(pl.multiple_of(offset + start, 8), size), :]

    def core_copy(tick, upper):
        return pltpu.make_async_remote_copy(
            src_ref=rows_of(tick, 2 * upper + 1, 0, chunk),
            dst_ref=core_in.at[tick, upper],
            send_sem=core_send.at[tick, upper],
            recv_sem=core_recv.at[tick, upper],
            device_id=at(1),
            device_id_type=pl.DeviceIdType.MESH,
        )

    def first_bit(upper, side):
        for position, bit in enumerate(orders[side]):
            if upper >> (bit - 1) & 1:
                return position, bit
        return len(orders[side]), None

    def stage_copy(tick, upper, side):
        _, bit = first_bit(upper, side)
        return pltpu.make_async_remote_copy(
            src_ref=rows_of(tick, 2 * upper, side * half, half),
            dst_ref=stage_in.at[tick, upper - 1, side],
            send_sem=stage_send.at[tick, upper - 1, side],
            recv_sem=stage_recv.at[tick, upper - 1, side],
            device_id=at(1 << bit),
            device_id_type=pl.DeviceIdType.MESH,
        )

    def hop_copy(side):
        return pltpu.make_async_remote_copy(
            src_ref=out_ref.at[0, 0, pl.ds(side * half, half), :],
            dst_ref=hop_in.at[pl.ds(side * half, half), :],
            send_sem=hop_send.at[side],
            recv_sem=hop_recv.at[side],
            device_id={"site": site + 1},
            device_id_type=pl.DeviceIdType.MESH,
        )

    def settle(tick, upper):
        core_copy(tick, upper).wait_recv()
        sides = sorted(range(2), key=lambda side: first_bit(upper, side)[0])
        for side in sides:
            position, bit = first_bit(upper, side)
            own = rows_of(tick, 2 * upper, side * half, half)
            total = own[...] + core_in[tick, upper, pl.ds(side * half, half), :]
            for earlier in orders[side][:position]:
                source = upper | 1 << (earlier - 1)
                stage_copy(tick, source, side).wait_recv()
                total = total + stage_in[tick, source - 1, side]
            if bit is None:
                out_ref[0, tick, pl.ds(side * half, half), :] = total
                if tick == 0:

                    @pl.when(site < sites - 1)
                    def _():
                        hop_copy(side).start()

            else:
                own[...] = total
                stage_copy(tick, upper, side).start()

    def greet():
        edges = (site > 0).astype(jnp.int32) + (site < sites - 1).astype(jnp.int32)
        pl.semaphore_wait(barrier, bits + edges)

    for tick in range(ticks):
        if tick == 0:
            prepare(panel_ref[0], 0)
        else:

            @pl.when(site == 0)
            def _():
                hop_in[...] = fresh_ref[tick - 1]

            @pl.when(site > 0)
            def _():
                for side in range(2):
                    hop_copy(side).wait_recv()

            prepare(hop_in[...], tick)
        group = per_block // 2
        pending = []
        for step in range(blocks):
            compute(tick, step)
            if tick == 0 and step == 0:
                greet()
            block = blocks - 1 - step
            ready = [block * group + inner for inner in reversed(range(group))]
            for upper in ready:
                core_copy(tick, upper).start()
            for upper in pending:
                settle(tick, upper)
            pending = ready
        for upper in pending:
            settle(tick, upper)

    for tick in range(ticks):
        for upper in range(uppers):
            core_copy(tick, upper).wait_send()
            if upper:
                for side in range(2):
                    stage_copy(tick, upper, side).wait_send()

    @pl.when(site < sites - 1)
    def _():
        for side in range(2):
            hop_copy(side).wait_send()


def on_device(sites, bond, site_tensor, panels, fresh, outcomes):
    _, count, rows, columns = site_tensor.shape
    samples = panels.shape[2]
    ticks = outcomes.shape[1]
    chunk = columns // bond
    width = math.lcm(TILE, 2 * chunk)
    blocks = columns // width
    tiles = columns // TILE
    depth = count * rows
    uppers = bond // 2
    half = chunk // 2
    plan = (sites, bond, ticks, count, rows, samples, chunk, width)
    dma = pltpu.SemaphoreType.DMA
    return pl.pallas_call(
        functools.partial(kernel, plan),
        out_shape=jax.ShapeDtypeStruct((1, ticks, chunk, samples), jnp.float32),
        in_specs=[pl.BlockSpec(memory_space=pl.ANY)]
        + [pl.BlockSpec(memory_space=pltpu.VMEM)] * 3,
        out_specs=pl.BlockSpec(memory_space=pltpu.VMEM),
        scratch_shapes=[
            pltpu.VMEM((tiles, count, rows, TILE), jnp.float32),
            pltpu.VMEM((tiles, depth, TILE), jnp.bfloat16),
            pltpu.VMEM((tiles, depth, TILE), jnp.bfloat16),
            pltpu.VMEM((depth, samples), jnp.float32),
            pltpu.VMEM((2 * samples, depth), jnp.bfloat16),
            pltpu.VMEM((ticks, blocks, width, samples), jnp.float32),
            pltpu.VMEM((ticks, uppers, chunk, samples), jnp.float32),
            pltpu.VMEM((ticks, uppers - 1, 2, half, samples), jnp.float32),
            pltpu.VMEM((chunk, samples), jnp.float32),
            dma((tiles,)),
            dma((ticks, uppers)),
            dma((ticks, uppers)),
            dma((ticks, uppers - 1, 2)),
            dma((ticks, uppers - 1, 2)),
            dma((2,)),
            dma((2,)),
        ],
        compiler_params=pltpu.CompilerParams(
            collective_id=0, has_side_effects=True, vmem_limit_bytes=60 * 1024 * 1024
        ),
        name="window",
    )(site_tensor, panels, fresh, outcomes)


def solution(mesh):
    placed = (
        P("site", None, "bond", None),
        P("site", "bond", None),
        P(None, "bond", None),
        P("site", None, None),
    )
    return jax.shard_map(
        functools.partial(on_device, mesh.shape["site"], mesh.shape["bond"]),
        mesh=mesh,
        in_specs=placed,
        out_specs=P("site", None, "bond", None),
        check_vma=False,
    )
```

```python
import functools
import math

import jax
import jax.numpy as jnp
from jax import lax
from jax.experimental import pallas as pl
from jax.experimental.pallas import tpu as pltpu
from jax.sharding import PartitionSpec as P

TILE = 256
LANES = 128


def flipped(index, mask):
    result = index
    bit = 0
    while (1 << bit) <= mask:
        if mask >> bit & 1:
            result = result + (1 - 2 * ((index // (1 << bit)) % 2)) * (1 << bit)
        bit += 1
    return result


def kernel(
    plan,
    tensor_ref,
    panel_ref,
    fresh_ref,
    outcome_ref,
    out_ref,
    raw,
    high,
    low,
    stacked,
    left,
    part,
    core_in,
    stage_in,
    hop_in,
    panel,
    done,
    panel_sem,
    fresh_sem,
    done_sem,
    load_sem,
    core_send,
    core_recv,
    stage_send,
    stage_recv,
    hop_send,
    hop_recv,
):
    sites, bond, ticks, count, rows, samples, chunk, width = plan
    bits = bond.bit_length() - 1
    uppers = 1 << (bits - 1)
    per_block = width // chunk
    blocks = bond // per_block
    tiles = width // TILE
    half = chunk // 2
    orders = (tuple(range(1, bits)), tuple(reversed(range(1, bits))))

    me = lax.axis_index("bond")
    site = lax.axis_index("site")

    def at(bond_mask):
        return {"bond": flipped(me, bond_mask)}

    def load(step, tile):
        block = flipped(me // per_block, blocks - 1 - step)
        column = pl.multiple_of(block * width + tile * TILE, TILE)
        return pltpu.make_async_copy(
            tensor_ref.at[0, :, :, pl.ds(column, TILE)],
            raw.at[step * tiles + tile],
            load_sem.at[step * tiles + tile],
        )

    panel_load = pltpu.make_async_copy(panel_ref.at[0], panel, panel_sem)
    panel_load.start()
    for step in range(blocks):
        for tile in range(tiles):
            load(step, tile).start()
    fresh_load = pltpu.make_async_copy(fresh_ref.at[0], hop_in, fresh_sem)

    @pl.when(site == 0)
    def _():
        fresh_load.start()

    barrier = pltpu.get_barrier_semaphore()
    for bit in range(bits):
        pl.semaphore_signal(
            barrier, inc=1, device_id=at(1 << bit), device_id_type=pl.DeviceIdType.MESH
        )

    @pl.when(site > 0)
    def _():
        pl.semaphore_signal(
            barrier, inc=1, device_id={"site": site - 1}, device_id_type=pl.DeviceIdType.MESH
        )

    @pl.when(site < sites - 1)
    def _():
        pl.semaphore_signal(
            barrier, inc=1, device_id={"site": site + 1}, device_id_type=pl.DeviceIdType.MESH
        )

    def prepare(vectors, tick):
        chosen = outcome_ref[0, pl.ds(tick, 1), :]

        def put(turned, start):
            upper = turned.astype(jnp.bfloat16)
            span = pl.ds(start, turned.shape[1])
            left[pl.ds(0, samples), span] = upper
            left[pl.ds(samples, samples), span] = (turned - upper.astype(jnp.float32)).astype(
                jnp.bfloat16
            )

        if rows % LANES == 0:
            whose = jnp.broadcast_to(chosen.astype(jnp.float32), (LANES, samples)).T
            for first in range(0, rows, LANES):
                turned = vectors[first : first + LANES].T
                for outcome in range(count):
                    put(jnp.where(whose == outcome, turned, 0.0), outcome * rows + first)
        else:
            for outcome in range(count):
                stacked[pl.ds(outcome * rows, rows), :] = jnp.where(chosen == outcome, vectors, 0.0)
            put(stacked[...].T, 0)

    def compute(tick, step):
        def one(tile):
            index = step * tiles + tile
            if tick == 0:
                load(step, tile).wait()
                for outcome in range(count):
                    values = raw[index, outcome]
                    upper = values.astype(jnp.bfloat16)
                    high[index, pl.ds(outcome * rows, rows), :] = upper
                    low[index, pl.ds(outcome * rows, rows), :] = (
                        values - upper.astype(jnp.float32)
                    ).astype(jnp.bfloat16)
            both = jnp.dot(left[...], high[index], preferred_element_type=jnp.float32)
            rest = jnp.dot(
                left[pl.ds(0, samples), :], low[index], preferred_element_type=jnp.float32
            )
            total = both[:samples] + (both[samples:] + rest)
            part[tick, step, pl.ds(pl.multiple_of(tile * TILE, TILE), TILE), :] = total.T

        if plan_unroll:
            for tile in range(tiles):
                one(tile)
        else:
            lax.fori_loop(0, tiles, lambda tile, _: (one(tile), 0)[1], 0)

    plan_unroll = True

    def place(rel):
        step = blocks - 1 - rel // per_block
        offset = flipped(me % per_block, rel % per_block) * chunk
        return step, offset

    def rows_of(tick, rel, start, size):
        step, offset = place(rel)
        return part.at[tick, step, pl.ds(pl.multiple_of(offset + start, 8), size), :]

    def core_copy(tick, upper):
        return pltpu.make_async_remote_copy(
            src_ref=rows_of(tick, 2 * upper + 1, 0, chunk),
            dst_ref=core_in.at[tick, upper],
            send_sem=core_send.at[tick, upper],
            recv_sem=core_recv.at[tick, upper],
            device_id=at(1),
            device_id_type=pl.DeviceIdType.MESH,
        )

    def first_bit(upper, side):
        for position, bit in enumerate(orders[side]):
            if upper >> (bit - 1) & 1:
                return position, bit
        return len(orders[side]), None

    def stage_copy(tick, upper, side):
        _, bit = first_bit(upper, side)
        return pltpu.make_async_remote_copy(
            src_ref=rows_of(tick, 2 * upper, side * half, half),
            dst_ref=stage_in.at[tick, upper - 1, side],
            send_sem=stage_send.at[tick, upper - 1, side],
            recv_sem=stage_recv.at[tick, upper - 1, side],
            device_id=at(1 << bit),
            device_id_type=pl.DeviceIdType.MESH,
        )

    def hop_copy(side):
        return pltpu.make_async_remote_copy(
            src_ref=done.at[0, pl.ds(side * half, half), :],
            dst_ref=hop_in.at[pl.ds(side * half, half), :],
            send_sem=hop_send.at[side],
            recv_sem=hop_recv.at[side],
            device_id={"site": site + 1},
            device_id_type=pl.DeviceIdType.MESH,
        )

    def store(tick, side):
        span = pl.ds(side * half, half)
        return pltpu.make_async_copy(
            done.at[tick, span, :], out_ref.at[0, tick, span, :], done_sem.at[tick, side]
        )

    def settle(tick, upper):
        core_copy(tick, upper).wait_recv()
        sides = sorted(range(2), key=lambda side: first_bit(upper, side)[0])
        for side in sides:
            position, bit = first_bit(upper, side)
            own = rows_of(tick, 2 * upper, side * half, half)
            total = own[...] + core_in[tick, upper, pl.ds(side * half, half), :]
            for earlier in orders[side][:position]:
                source = upper | 1 << (earlier - 1)
                stage_copy(tick, source, side).wait_recv()
                total = total + stage_in[tick, source - 1, side]
            if bit is None:
                done[tick, pl.ds(side * half, half), :] = total
                if tick == 0:

                    @pl.when(site < sites - 1)
                    def _():
                        hop_copy(side).start()

                store(tick, side).start()
            else:
                own[...] = total
                stage_copy(tick, upper, side).start()

    def greet():
        edges = (site > 0).astype(jnp.int32) + (site < sites - 1).astype(jnp.int32)
        pl.semaphore_wait(barrier, bits + edges)

    for tick in range(ticks):
        if tick == 0:
            panel_load.wait()
            prepare(panel[...], 0)
        else:

            @pl.when(site == 0)
            def _():
                fresh_load.wait()

            @pl.when(site > 0)
            def _():
                for side in range(2):
                    hop_copy(side).wait_recv()

            prepare(hop_in[...], tick)
        group = per_block // 2
        pending = []
        for step in range(blocks):
            compute(tick, step)
            if tick == 0 and step == 0:
                greet()
            block = blocks - 1 - step
            ready = [block * group + inner for inner in reversed(range(group))]
            for upper in ready:
                core_copy(tick, upper).start()
            for upper in pending:
                settle(tick, upper)
            pending = ready
        for upper in pending:
            settle(tick, upper)

    for tick in range(ticks):
        for upper in range(uppers):
            core_copy(tick, upper).wait_send()
            if upper:
                for side in range(2):
                    stage_copy(tick, upper, side).wait_send()
        for side in range(2):
            store(tick, side).wait()

    @pl.when(site < sites - 1)
    def _():
        for side in range(2):
            hop_copy(side).wait_send()


def on_device(sites, bond, site_tensor, panels, fresh, outcomes):
    _, count, rows, columns = site_tensor.shape
    samples = panels.shape[2]
    ticks = outcomes.shape[1]
    chunk = columns // bond
    width = math.lcm(TILE, 2 * chunk)
    blocks = columns // width
    tiles = columns // TILE
    depth = count * rows
    uppers = bond // 2
    half = chunk // 2
    plan = (sites, bond, ticks, count, rows, samples, chunk, width)
    dma = pltpu.SemaphoreType.DMA
    return pl.pallas_call(
        functools.partial(kernel, plan),
        out_shape=jax.ShapeDtypeStruct((1, ticks, chunk, samples), jnp.float32),
        in_specs=[pl.BlockSpec(memory_space=pl.ANY)] * 3
        + [pl.BlockSpec(memory_space=pltpu.VMEM)],
        out_specs=pl.BlockSpec(memory_space=pl.ANY),
        scratch_shapes=[
            pltpu.VMEM((tiles, count, rows, TILE), jnp.float32),
            pltpu.VMEM((tiles, depth, TILE), jnp.bfloat16),
            pltpu.VMEM((tiles, depth, TILE), jnp.bfloat16),
            pltpu.VMEM((depth, samples), jnp.float32),
            pltpu.VMEM((2 * samples, depth), jnp.bfloat16),
            pltpu.VMEM((ticks, blocks, width, samples), jnp.float32),
            pltpu.VMEM((ticks, uppers, chunk, samples), jnp.float32),
            pltpu.VMEM((ticks, uppers - 1, 2, half, samples), jnp.float32),
            pltpu.VMEM((chunk, samples), jnp.float32),
            pltpu.VMEM((rows, samples), jnp.float32),
            pltpu.VMEM((ticks, chunk, samples), jnp.float32),
            dma,
            dma,
            dma((ticks, 2)),
            dma((tiles,)),
            dma((ticks, uppers)),
            dma((ticks, uppers)),
            dma((ticks, uppers - 1, 2)),
            dma((ticks, uppers - 1, 2)),
            dma((2,)),
            dma((2,)),
        ],
        compiler_params=pltpu.CompilerParams(
            collective_id=0, has_side_effects=True, vmem_limit_bytes=60 * 1024 * 1024
        ),
        name="window",
    )(site_tensor, panels, fresh, outcomes)


def solution(mesh):
    placed = (
        P("site", None, "bond", None),
        P("site", "bond", None),
        P(None, "bond", None),
        P("site", None, None),
    )
    return jax.shard_map(
        functools.partial(on_device, mesh.shape["site"], mesh.shape["bond"]),
        mesh=mesh,
        in_specs=placed,
        out_specs=P("site", None, "bond", None),
        check_vma=False,
    )
```

```python
import functools
import math

import jax
import jax.numpy as jnp
from jax import lax
from jax.experimental import pallas as pl
from jax.experimental.pallas import tpu as pltpu
from jax.sharding import PartitionSpec as P

TILE = 256
LANES = 128


def flipped(index, mask):
    result = index
    bit = 0
    while (1 << bit) <= mask:
        if mask >> bit & 1:
            result = result + (1 - 2 * ((index // (1 << bit)) % 2)) * (1 << bit)
        bit += 1
    return result


CORE_LAG = 1
LINK_LAG = 2


class Layout:
    def __init__(self, bond, columns):
        self.chunk = columns // bond
        self.tiles = columns // TILE
        self.uppers = bond // 2
        self.bits = bond.bit_length() - 1
        if self.chunk % LANES == 0:
            self.pieces, self.per_block = self.chunk // LANES, 2
            self.size = LANES
            self.split()
            pairs = [(upper, piece) for upper in range(self.uppers) for piece in range(self.pieces)]
            self.items = [[pair] for pair in sorted(pairs, key=self.rank)]
            self.group = self.pieces
        else:
            self.pieces, self.size = 1, self.chunk
            self.split()
            width = math.lcm(TILE, 2 * self.chunk)
            self.per_block = width // self.chunk
            self.group = self.block_tiles = width // TILE
            group = self.per_block // 2
            self.items = []
            for block in reversed(range(bond // self.per_block)):
                self.items += [[] for _ in range(self.block_tiles - 1)]
                self.items.append(
                    [(block * group + inner, 0) for inner in reversed(range(group))]
                )
        self.when = {item: tile for tile, items in enumerate(self.items) for item in items}

    def split(self):
        self.strands = []
        for piece in range(self.pieces):
            if 2 * piece + 1 == self.pieces:
                half = self.size // 2
                self.strands += [(piece, 0, half, False), (piece, half, half, True)]
            else:
                self.strands.append((piece, 0, self.size, 2 * piece >= self.pieces))

    def rank(self, pair):
        upper, piece = pair
        strands = self.strands_of(piece)
        late = sum(len(self.path(upper, strand)[0]) for strand in strands) / len(strands)
        middle = -abs(2 * piece + 1 - self.pieces)
        return -upper.bit_count(), late, middle, upper, piece

    def column(self, me, tile, part):
        if self.chunk % LANES == 0:
            ((upper, piece),) = self.items[tile]
            return (2 * flipped(me // 2, upper) + part) * self.chunk + piece * LANES
        step = tile // self.block_tiles
        block = flipped(me // self.per_block, self.tiles // self.block_tiles - 1 - step)
        width = self.block_tiles * TILE
        return block * width + tile % self.block_tiles * TILE + part * LANES

    def row(self, me, rel, piece):
        offset = flipped(me % self.per_block, rel % self.per_block) * self.size
        tile = self.when[rel // 2, piece]
        if self.chunk % LANES == 0:
            return tile * TILE + offset
        return tile // self.block_tiles * self.block_tiles * TILE + offset

    def path(self, upper, strand):
        order = list(range(1, self.bits))
        if self.strands[strand][3]:
            order.reverse()
        earlier = []
        for bit in order:
            if upper >> (bit - 1) & 1:
                return earlier, bit
            earlier.append(bit)
        return earlier, None

    def strands_of(self, piece):
        return [strand for strand, entry in enumerate(self.strands) if entry[0] == piece]

    def events(self):
        found, sent = [], {}
        for tile, items in enumerate(self.items):
            for upper, piece in items:
                pair = (tile // self.group + CORE_LAG, 0)
                found.append((pair, 0, upper, piece, None))
                for strand in self.strands_of(piece):
                    earlier, _ = self.path(upper, strand)
                    moment = pair
                    for bit in earlier:
                        source = sent[upper | 1 << (bit - 1), strand]
                        moment = max(moment, (source[0] + LINK_LAG, 1))
                    sent[upper, strand] = moment
                    if earlier:
                        found.append((moment, 1, upper, piece, strand))
        return sorted(found, key=lambda event: event[:2])


def kernel(
    plan,
    tensor_ref,
    panel_ref,
    fresh_ref,
    outcome_ref,
    out_ref,
    raw,
    high,
    low,
    stacked,
    left,
    part,
    core_in,
    stage_in,
    hop_in,
    load_sem,
    core_send,
    core_recv,
    stage_send,
    stage_recv,
    hop_send,
    hop_recv,
):
    layout, sites, ticks, count, rows, samples = plan
    me = lax.axis_index("bond")
    site = lax.axis_index("site")
    mesh_id = pl.DeviceIdType.MESH

    def at(mask):
        return {"bond": flipped(me, mask)}

    def load(tile, side):
        column = pl.multiple_of(layout.column(me, tile, side), LANES)
        return pltpu.make_async_copy(
            tensor_ref.at[0, :, :, pl.ds(column, LANES)],
            raw.at[tile, :, :, pl.ds(side * LANES, LANES)],
            load_sem.at[tile, side],
        )

    for tile in range(layout.tiles):
        for side in range(2):
            load(tile, side).start()
    barrier = pltpu.get_barrier_semaphore()
    for bit in range(layout.bits):
        pl.semaphore_signal(barrier, inc=1, device_id=at(1 << bit), device_id_type=mesh_id)

    @pl.when(site > 0)
    def _():
        pl.semaphore_signal(barrier, inc=1, device_id={"site": site - 1}, device_id_type=mesh_id)

    @pl.when(site < sites - 1)
    def _():
        pl.semaphore_signal(barrier, inc=1, device_id={"site": site + 1}, device_id_type=mesh_id)

    def greet():
        edges = (site > 0).astype(jnp.int32) + (site < sites - 1).astype(jnp.int32)
        pl.semaphore_wait(barrier, layout.bits + edges)

    def put(turned, start, size):
        upper = turned.astype(jnp.bfloat16)
        left[pl.ds(0, samples), pl.ds(start, size)] = upper
        left[pl.ds(samples, samples), pl.ds(start, size)] = (
            turned - upper.astype(jnp.float32)
        ).astype(jnp.bfloat16)

    def prepare(vectors, tick, piece):
        chosen = outcome_ref[0, pl.ds(tick, 1), :]
        if layout.size % LANES == 0:
            turned = vectors.T
            whose = jnp.broadcast_to(chosen.astype(jnp.float32), (LANES, samples)).T
            for outcome in range(count):
                start = outcome * rows + piece * LANES
                put(jnp.where(whose == outcome, turned, 0.0), start, LANES)
        else:
            for outcome in range(count):
                stacked[pl.ds(outcome * rows, rows), :] = jnp.where(chosen == outcome, vectors, 0.0)
            put(stacked[...].T, 0, count * rows)

    def compute(tick, tile):
        if tick == 0:
            for outcome in range(count):
                values = raw[tile, outcome]
                upper = values.astype(jnp.bfloat16)
                high[tile, pl.ds(outcome * rows, rows), :] = upper
                low[tile, pl.ds(outcome * rows, rows), :] = (
                    values - upper.astype(jnp.float32)
                ).astype(jnp.bfloat16)
        both = jnp.dot(left[...], high[tile], preferred_element_type=jnp.float32)
        rest = jnp.dot(left[pl.ds(0, samples), :], low[tile], preferred_element_type=jnp.float32)
        total = both[:samples] + (both[samples:] + rest)
        part[tick, pl.ds(tile * TILE, TILE), :] = total.T

    def rows_of(tick, rel, piece, start, size):
        row = pl.multiple_of(layout.row(me, rel, piece) + start, 8)
        return part.at[tick, pl.ds(row, size), :]

    def core_copy(tick, upper, piece):
        return pltpu.make_async_remote_copy(
            src_ref=rows_of(tick, 2 * upper + 1, piece, 0, layout.size),
            dst_ref=core_in.at[tick, upper, piece],
            send_sem=core_send.at[tick, upper, piece],
            recv_sem=core_recv.at[tick, upper, piece],
            device_id=at(1),
            device_id_type=mesh_id,
        )

    def stage_copy(tick, upper, strand):
        piece, start, size, _ = layout.strands[strand]
        _, bit = layout.path(upper, strand)
        return pltpu.make_async_remote_copy(
            src_ref=rows_of(tick, 2 * upper, piece, start, size),
            dst_ref=stage_in.at[tick, upper - 1, pl.ds(piece * layout.size + start, size), :],
            send_sem=stage_send.at[tick, upper - 1, strand],
            recv_sem=stage_recv.at[tick, upper - 1, strand],
            device_id=at(1 << bit),
            device_id_type=mesh_id,
        )

    def span_of(strand):
        piece, start, size, _ = layout.strands[strand]
        return pl.ds(piece * layout.size + start, size)

    def hop_copy(tick, strand):
        return pltpu.make_async_remote_copy(
            src_ref=out_ref.at[0, tick, span_of(strand), :],
            dst_ref=hop_in.at[tick, span_of(strand), :],
            send_sem=hop_send.at[tick, strand],
            recv_sem=hop_recv.at[tick, strand],
            device_id={"site": site + 1},
            device_id_type=mesh_id,
        )

    def settle(tick, event):
        _, kind, upper, piece, strand = event
        if kind == 0:
            core_copy(tick, upper, piece).wait_recv()
            own = rows_of(tick, 2 * upper, piece, 0, layout.size)
            own[...] += core_in[tick, upper, piece]
            for strand in layout.strands_of(piece):
                if upper and not layout.path(upper, strand)[0]:
                    stage_copy(tick, upper, strand).start()
            return
        earlier, bit = layout.path(upper, strand)
        _, start, size, _ = layout.strands[strand]
        own = rows_of(tick, 2 * upper, piece, start, size)
        total = own[...]
        for before in earlier:
            source = upper | 1 << (before - 1)
            stage_copy(tick, source, strand).wait_recv()
            total = total + stage_in[tick, source - 1, span_of(strand), :]
        if bit is not None:
            own[...] = total
            stage_copy(tick, upper, strand).start()
            return
        out_ref[0, tick, span_of(strand), :] = total
        if tick + 1 < ticks:

            @pl.when(site < sites - 1)
            def _():
                hop_copy(tick, strand).start()

    for tick in range(ticks):
        for piece in range(layout.pieces):
            span = pl.ds(piece * layout.size, layout.size)
            if tick == 0:
                prepare(panel_ref[0, span, :], tick, piece)
                continue

            @pl.when(site == 0)
            def _():
                hop_in[tick - 1, span, :] = fresh_ref[tick - 1, span, :]

            @pl.when(site > 0)
            def _():
                for strand in layout.strands_of(piece):
                    hop_copy(tick - 1, strand).wait_recv()

            prepare(hop_in[tick - 1, span, :], tick, piece)
        pending = layout.events()
        for first in range(0, layout.tiles, layout.group):
            members = range(first, first + layout.group)
            if tick == 0:
                for tile in members:
                    for side in range(2):
                        load(tile, side).wait()
            for tile in members:
                compute(tick, tile)
            if tick == 0 and first == 0:
                greet()
            for tile in members:
                for upper, piece in layout.items[tile]:
                    core_copy(tick, upper, piece).start()
            while pending and pending[0][0][0] <= first // layout.group:
                settle(tick, pending.pop(0))
        for event in pending:
            settle(tick, event)

    strands = range(len(layout.strands))
    for tick in range(ticks):
        for upper in range(layout.uppers):
            for piece in range(layout.pieces):
                core_copy(tick, upper, piece).wait_send()
            if upper:
                for strand in strands:
                    stage_copy(tick, upper, strand).wait_send()

    @pl.when(site < sites - 1)
    def _():
        for tick in range(ticks - 1):
            for strand in strands:
                hop_copy(tick, strand).wait_send()


def on_device(sites, bond, site_tensor, panels, fresh, outcomes):
    _, count, rows, columns = site_tensor.shape
    samples = panels.shape[2]
    ticks = outcomes.shape[1]
    layout = Layout(bond, columns)
    tiles, uppers, pieces = layout.tiles, layout.uppers, layout.pieces
    chunk, size, strands = layout.chunk, layout.size, len(layout.strands)
    depth = count * rows
    dma = pltpu.SemaphoreType.DMA
    return pl.pallas_call(
        functools.partial(kernel, (layout, sites, ticks, count, rows, samples)),
        out_shape=jax.ShapeDtypeStruct((1, ticks, chunk, samples), jnp.float32),
        in_specs=[pl.BlockSpec(memory_space=pl.ANY)]
        + [pl.BlockSpec(memory_space=pltpu.VMEM)] * 3,
        out_specs=pl.BlockSpec(memory_space=pltpu.VMEM),
        scratch_shapes=[
            pltpu.VMEM((tiles, count, rows, TILE), jnp.float32),
            pltpu.VMEM((tiles, depth, TILE), jnp.bfloat16),
            pltpu.VMEM((tiles, depth, TILE), jnp.bfloat16),
            pltpu.VMEM((depth, samples), jnp.float32),
            pltpu.VMEM((2 * samples, depth), jnp.bfloat16),
            pltpu.VMEM((ticks, columns, samples), jnp.float32),
            pltpu.VMEM((ticks, uppers, pieces, size, samples), jnp.float32),
            pltpu.VMEM((ticks, uppers - 1, chunk, samples), jnp.float32),
            pltpu.VMEM((ticks - 1, chunk, samples), jnp.float32),
            dma((tiles, 2)),
            dma((ticks, uppers, pieces)),
            dma((ticks, uppers, pieces)),
            dma((ticks, uppers - 1, strands)),
            dma((ticks, uppers - 1, strands)),
            dma((ticks - 1, strands)),
            dma((ticks - 1, strands)),
        ],
        compiler_params=pltpu.CompilerParams(
            collective_id=0, has_side_effects=True, vmem_limit_bytes=60 * 1024 * 1024
        ),
        name="window",
    )(site_tensor, panels, fresh, outcomes)


def solution(mesh):
    placed = (
        P("site", None, "bond", None),
        P("site", "bond", None),
        P(None, "bond", None),
        P("site", None, None),
    )
    return jax.shard_map(
        functools.partial(on_device, mesh.shape["site"], mesh.shape["bond"]),
        mesh=mesh,
        in_specs=placed,
        out_specs=P("site", None, "bond", None),
        check_vma=False,
    )
```
